32 devices in a mesh: clients: 8 (over z, x), mp: 4 (over y, core).
Axes of the slice: x: 2, y: 2, z: 4, core: 2. Of those that a mesh axis runs over, the one named last changes fastest.
Arguments:
- inputs: bfloat16 [8, 256, 2048], P('clients'), may hold values from -6 to 6
- targets: bfloat16 [8, 256, 2048], P('clients'), may hold values from -6 to 6
- local_steps: int32 [8], P('clients'), may hold values from 1 to 2, as said below
- sample_counts: int32 [8], P('clients'), may hold values from 100 to 600
- weight_in: bfloat16 [2048, 7168], P('clients', 'mp'), may hold values from -0.125 to 0.125
- weight_out: bfloat16 [7168, 2048], P('mp', 'clients'), may hold values from -0.0625 to 0.0625
Outputs:
- update_in: float32 [2048, 7168], P('clients', 'mp')
- update_out: float32 [7168, 2048], P('mp', 'clients')
The draws below stay inside these ranges and needn't reach their ends.
Inputs may be any that keep to these rules, and one draw needn't show every extreme that they name: `local_steps`: some client has exactly 2 steps.
All inputs are finite; a program needn't handle non-finite values.
Results may differ from the reference program's by a relative error of at most 0.017.
Values may be sent and summed in bfloat16 or wider, within the bound.
No kernel may reach another device: no remote copies, remote signals or barrier semaphores. Data moves between devices by JAX's collectives and lax.ppermute only.
A program may use at most 128 MiB of HBM per device.

```python
import jax
import jax.numpy as jnp
from jax import lax

D = 2048
FF = 7168
ROWS = 256
TAU_MAX = 2
CLIENTS = 8


def draw_local_steps(key, part):
    first = jax.random.fold_in(key, 11)
    second = jax.random.fold_in(key, 12)
    levels = jax.random.randint(first, (CLIENTS,), 0, 10)
    counts = jnp.where(levels < 7, 1, jnp.where(levels == 7, 2, 3))
    counts = jnp.minimum(counts, TAU_MAX)
    where_max = jax.random.randint(second, (), 0, CLIENTS)
    counts = jnp.where(jnp.arange(CLIENTS) == where_max, TAU_MAX, counts)
    return counts.astype(jnp.int32)


def draw_sample_counts(key, part):
    first = jax.random.fold_in(key, 21)
    base = jax.random.randint(first, (CLIENTS,), 100, 201)
    ramp = CLIENTS - 1 + 2 * jnp.arange(CLIENTS)
    counts = base * ramp // (CLIENTS - 1)
    places = jnp.arange(CLIENTS)
    counts = jnp.where(places == CLIENTS - 1, 600, counts)
    counts = jnp.where(places == 0, 100, counts)
    return counts.astype(jnp.int32)


def shard_levels(key, shape, cuts, low, high):
    def one(position, blocks):
        steps = jax.random.uniform(jax.random.fold_in(jax.random.fold_in(key, 6), position), (blocks,), jnp.float32, low / len(cuts), high / len(cuts))
        return jnp.repeat(jnp.exp(steps), shape[position] // blocks).reshape((-1,) + (1,) * (len(shape) - position - 1))

    level = one(*cuts[0])
    for cut in cuts[1:]:
        level = level * one(*cut)
    return level


def centred(key, extent, deviation, reach, split=(), dtype=jnp.bfloat16):
    level = shard_levels(key, extent, split, -0.22, 0.18) if split else 1.0
    drawn = jax.random.normal(key, extent, jnp.float32) * deviation * level
    return jnp.minimum(jnp.maximum(drawn, -reach), reach).astype(dtype)


def setup_inputs(seed: int = 0) -> dict:
    key_list = jax.random.split(jax.random.key(seed), 7)
    return {
        "inputs": centred(key_list[0], (CLIENTS, ROWS, D), 1.0, 6.0, ((0, 8),)),
        "targets": centred(key_list[1], (CLIENTS, ROWS, D), 1.0, 6.0, ((0, 8),)),
        "local_steps": draw_local_steps(jax.random.fold_in(key_list[6], 71), 0),
        "sample_counts": draw_sample_counts(jax.random.fold_in(key_list[6], 71), 0),
        "weight_in": centred(key_list[4], (D, FF), D ** -0.5, 0.125, ((0, 8), (1, 4))),
        "weight_out": centred(key_list[5], (FF, D), FF ** -0.5, 0.0625, ((0, 4), (1, 8))),
    }


learn_rate = 0.005
loss_scale = 0.0625


def train_client(tokens, wanted, count, start_in, start_out):
    local_in = start_in.astype(jnp.float32)
    local_out = start_out.astype(jnp.float32)
    for step_index in range(TAU_MAX):
        cur_in = local_in.astype(jnp.bfloat16)
        cur_out = local_out.astype(jnp.bfloat16)
        pre = jnp.dot(tokens, cur_in, preferred_element_type=jnp.float32)
        hidden = jax.nn.silu(pre).astype(jnp.bfloat16)
        output = jnp.dot(hidden, cur_out, preferred_element_type=jnp.float32)
        error = ((output - wanted.astype(jnp.float32)) * loss_scale).astype(jnp.bfloat16)
        grad_out = jnp.dot(hidden.T, error, preferred_element_type=jnp.float32)
        back = jnp.dot(error, cur_out.T, preferred_element_type=jnp.float32)
        sigma = jax.nn.sigmoid(pre)
        dpre = (back * sigma * (1.0 + pre * (1.0 - sigma))).astype(jnp.bfloat16)
        grad_in = jnp.dot(tokens.T, dpre, preferred_element_type=jnp.float32)
        active = step_index < count
        local_in = jnp.where(active, local_in - learn_rate * grad_in, local_in)
        local_out = jnp.where(active, local_out - learn_rate * grad_out, local_out)
    return local_in, local_out


def reference(inputs, targets, local_steps, sample_counts, weight_in, weight_out):
    base_in = weight_in.astype(jnp.float32)
    base_out = weight_out.astype(jnp.float32)

    def visit(carry, packed):
        tokens, wanted, count, samples = packed
        local_in, local_out = train_client(tokens, wanted, count, weight_in, weight_out)
        factor = samples.astype(jnp.float32) / (learn_rate * count.astype(jnp.float32))
        term_in = ((base_in - local_in) * factor).astype(jnp.bfloat16)
        term_out = ((base_out - local_out) * factor).astype(jnp.bfloat16)
        return (carry[0] + term_in.astype(jnp.float32), carry[1] + term_out.astype(jnp.float32)), None

    zeros = (jnp.zeros(weight_in.shape, jnp.float32), jnp.zeros(weight_out.shape, jnp.float32))
    summed, unused = lax.scan(visit, zeros, (inputs, targets, local_steps, sample_counts))
    ntot = jnp.sum(sample_counts.astype(jnp.float32))
    ntau = jnp.sum((sample_counts * local_steps).astype(jnp.float32))
    scale = ntau / (ntot * ntot)
    return summed[0] * scale, summed[1] * scale
```

```python
import itertools

import jax
import jax.numpy as jnp
from jax import lax
from jax.experimental import pallas as pl
from jax.experimental.pallas import tpu as pltpu
from jax.sharding import PartitionSpec as P

TAU_MAX = 2
CORES = 2
SIDES = 2
learn_rate = 0.005
loss_scale = 0.0625
f32 = jnp.float32
bf16 = jnp.bfloat16


def dot(a, b, ca, cb):
    return lax.dot_general(a, b, (((ca,), (cb,)), ((), ())), preferred_element_type=f32)


def cat(parts, axis=0):
    return parts[0] if len(parts) == 1 else jnp.concatenate(parts, axis=axis)


def make_plain(n_clients, n_mp):
    nc = CORES
    ny = n_mp // nc
    nx = max(d for d in range(1, n_clients + 1) if n_clients % d == 0 and d * d <= n_clients)
    nz = n_clients // nx
    nh = nz // SIDES
    groups = [(d, t) for d in range(nh) for t in range(nx)]
    peers = [(g, r) for g in range(SIDES) for r in range(ny)]

    def flat(h, s, x, y, c):
        return (((h % nh) * SIDES + s) * nx + x % nx) * n_mp + (y % ny) * nc + c

    def send(value, h=0, s=0, x=0, y=0, c=0):
        pairs = [
            (flat(a, b, d, e, k), flat(a + h, b ^ s, d + x, e + y, k ^ c))
            for a, b, d, e, k in itertools.product(range(nh), range(SIDES), range(nx), range(ny), range(nc))
        ]
        return lax.ppermute(value, ("clients", "mp"), pairs)

    def local(inputs, targets, local_steps, sample_counts, weight_in, weight_out):
        ci, mi = lax.axis_index("clients"), lax.axis_index("mp")
        z, x = ci // nx, ci % nx
        h, s = z // SIDES, z % SIDES
        y, c = mi // nc, mi % nc
        rows, width = inputs.shape[1:]
        rb = rows // n_mp
        blk = weight_in.shape[0]
        fm = weight_in.shape[1]
        ff = fm // SIDES
        part = ff // nh
        cols = [(d, f, t) for d in range(nh) for f in range(SIDES) for t in range(nx)]
        start = {
            (d, f, t): ((((h - d) % nh) * SIDES + (s ^ f)) * nx + (x - t) % nx) * blk for d, f, t in cols
        }
        own_row = mi * rb

        def gather(own, other):
            slots = {(0, 0, 0): own}
            for d in list(range(1, nh)) + [0]:
                for f in range(SIDES):
                    if (d, f) != (0, 0):
                        slots[d, f, 0] = send((own, other)[f], h=d, s=f)
            for d in range(nh):
                for f in range(SIDES):
                    for t in range(1, nx):
                        slots[d, f, t] = send(slots[d, f, 0], x=t)
            return slots

        w_in = gather(
            lax.dynamic_slice_in_dim(weight_in, s * ff, ff, 1),
            lax.dynamic_slice_in_dim(weight_in, (1 - s) * ff, ff, 1),
        )
        w_out = gather(
            lax.dynamic_slice_in_dim(weight_out, s * ff, ff, 0),
            lax.dynamic_slice_in_dim(weight_out, (1 - s) * ff, ff, 0),
        )

        def row_block(r, k):
            return lax.dynamic_slice_in_dim(inputs[0], (((y - r) % ny) * nc + (c ^ k)) * rb, rb, 0)

        mine = cat([row_block(r, 0) for r in range(ny)])
        theirs = send(mine, s=1)
        theirs_far = send(theirs, c=1)
        natural = cat(
            [row_block(r, k) for r in range(ny) for k in range(nc)]
            + [
                lax.slice_in_dim((theirs, theirs_far)[k], r * rb, (r + 1) * rb)
                for r in range(ny)
                for k in range(nc)
            ]
        )
        tokens = {j: lax.dynamic_slice_in_dim(natural, start[j], blk, 1) for j in cols}
        gram = [
            dot(natural[g * rows : (g + 1) * rows], natural[g * rows : (g + 1) * rows], 1, 1).astype(bf16)
            for g in range(SIDES)
        ]
        piece_u = lax.dynamic_slice_in_dim(inputs[0], own_row, rb, 0)
        piece_u = {j: lax.dynamic_slice_in_dim(piece_u, start[j], blk, 1) for j in cols}
        wanted = lax.dynamic_slice_in_dim(targets[0], own_row, rb, 0)
        wanted = {j: lax.dynamic_slice_in_dim(wanted, start[j], blk, 1) for j in cols}

        count, samples = local_steps[0], sample_counts[0]
        pair = jnp.broadcast_to(jnp.stack([samples, samples * count, count])[:, None], (3, 128))
        pair_far = send(pair, s=1)
        total = pair + pair_far
        total = sum([send(total, x=t) for t in range(1, nx)], total)
        total = sum([send(total, h=d) for d in range(1, nh)], total)
        ntot = total[0, 0].astype(f32)
        ntau = total[1, 0].astype(f32)
        scale = ntau / (ntot * ntot)
        counts = (count, pair_far[2, 0])
        factor = [
            n.astype(f32) / k.astype(f32) * scale for n, k in zip((samples, pair_far[0, 0]), counts)
        ]

        def by_client(values, width_):
            return cat([jnp.broadcast_to(v, (1, width_)) for v in values], 1)

        weight_row = by_client(factor, rows)

        def reduce_rows(partial, names):
            whole = cat([partial[j] for j in names], 1).reshape(SIDES * ny, nc, rb, -1)
            got = send(whole[:, 1].astype(bf16), c=1)
            near = whole[:, 0] + got.astype(f32)
            result = None
            for i, (g, r) in enumerate(peers):
                if (g, r) == (0, 0):
                    result = {j: near[i][:, n * blk : (n + 1) * blk] for n, j in enumerate(names)}
            for i, (g, r) in enumerate(peers):
                if (g, r) != (0, 0):
                    back = send(near[i].astype(bf16), s=g, y=-r).astype(f32)
                    back = {j: back[:, n * blk : (n + 1) * blk] for n, j in enumerate(names)}
                    result = {(d, f, t): result[d, f, t] + back[d, f ^ g, t] for d, f, t in names}
            return result

        def spread_rows(piece, flip):
            out = {(0, 0, 0): piece}
            for g, r in peers:
                if (g, r) != (0, 0):
                    back = send(piece, s=g, y=-r)
                    out[g, (-r) % ny, 0] = flip(back) if g else back
            far = send(cat([out[g, r, 0] for g, r in peers]), c=1)
            n = piece.shape[0]
            for i, (g, r) in enumerate(peers):
                out[g, r, 1] = far[i * n : (i + 1) * n]
            return out

        order = [(g, r, k) for g, r in peers for k in range(nc)]

        def flip_of(names):
            def flip(v):
                place = {j: n for n, j in enumerate(names)}
                return cat(
                    [v[:, place[d, f ^ 1, t] * blk : (place[d, f ^ 1, t] + 1) * blk] for d, f, t in names], 1
                )

            return flip

        def spread_error(error, names):
            got = spread_rows(cat([error[j] for j in names], 1), flip_of(names))
            whole = cat([got[o] for o in order])
            return {j: whole[:, n * blk : (n + 1) * blk] for n, j in enumerate(names)}

        lasts = [(d, f) for d in range(nh) for f in range(SIDES)]

        def spread_all(piece, near):
            got = []
            for d, t in groups:
                if (d, t) != (0, 0):
                    back = send(cat([piece[e, f, (-t) % nx] for e, f in lasts], 1), h=d, x=t)
                    got.append(
                        cat([back[:, i * blk : (i + 1) * blk] for i in [lasts.index(((e - d) % nh, f)) for e, f in lasts]], 1)
                    )
            got = spread_rows(cat(got), flip_of([(d, f, 0) for d, f in lasts]))
            whole = [near]
            for b in range(len(groups) - 1):
                whole += [got[o][b * rb : (b + 1) * rb] for o in order]
            return cat(whole)

        def near_columns(blocks):
            return cat([blocks[d, f, 0] for d, f in lasts], 1)

        def spread_hidden(v):
            near = {}
            for d in range(nh):
                own = lax.dynamic_slice_in_dim(v, ((h + d) % nh) * part, part, 0)
                near[d, 0] = send(own, h=d) if d else own
            for d in range(nh):
                for t in range(1, nx):
                    near[d, t] = send(near[d, 0], x=t)
            return cat([near[b] for b in groups], 1)

        pre = sum([dot(w_in[j], tokens[j], 0, 1) for j in cols[1:]], dot(w_in[cols[0]], tokens[cols[0]], 0, 1))
        hidden = jax.nn.silu(pre).astype(bf16)

        def errors(partial):
            summed = reduce_rows(partial, cols)
            return {j: (summed[j] - wanted[j].astype(f32)) * loss_scale for j in cols}

        def rounded(raw):
            return {j: raw[j].astype(bf16) for j in cols}

        def spread_errors(error):
            return spread_error(error, cols)

        def back_of(whole):
            parts = [dot(w_out[j], whole[j], 1, 1) for j in cols]
            return sum(parts[1:], parts[0])

        def slope(pre_):
            sigma = jax.nn.sigmoid(pre_)
            return sigma * (1.0 + pre_ * (1.0 - sigma))

        def clients(v):
            return [v[:, g * rows : (g + 1) * rows] for g in range(SIDES)]

        raw0 = errors({j: dot(hidden, w_out[j], 0, 0) for j in cols})
        error0 = spread_errors(rounded(raw0))
        dpre0 = (back_of(error0) * slope(pre)).astype(bf16)

        pre1 = pre - learn_rate * cat([dot(d, g, 1, 0) for d, g in zip(clients(dpre0), gram)], 1)
        hidden1 = jax.nn.silu(pre1).astype(bf16)
        cross = [dot(a, b, 0, 0).astype(bf16) for a, b in zip(clients(hidden1), clients(hidden))]

        def output1(j):
            change = cat([dot(m, error0[j][g * rows : (g + 1) * rows], 1, 0) for g, m in enumerate(cross)])
            return dot(hidden1, w_out[j], 0, 0) - learn_rate * change

        raw1 = errors({j: output1(j) for j in cols})
        error1 = spread_errors(rounded(raw1))
        between = [
            sum([dot(error0[j][g * rows : (g + 1) * rows], error1[j][g * rows : (g + 1) * rows], 1, 1) for j in cols]).astype(bf16)
            for g in range(SIDES)
        ]
        back1 = back_of(error1) - learn_rate * cat([dot(a, m, 1, 0) for a, m in zip(clients(hidden), between)], 1)
        dpre1 = (back1 * slope(pre1)).astype(bf16)

        active = [(k > 1).astype(f32) for k in counts]
        active_row = by_client(active, rows)
        moved = ((dpre0.astype(f32) + active_row * dpre1.astype(f32)) * weight_row).astype(bf16)
        own_factor = factor[0]
        near_weight = weight_row.reshape(-1, 1)

        def all_errors(raw, whole, act, act_row):
            piece = {j: (raw[j] * (own_factor * act)).astype(bf16) for j in cols}
            near = (near_columns(whole).astype(f32) * (near_weight * act_row)).astype(bf16)
            return spread_all(piece, near)

        tokens_all = spread_all(piece_u, near_columns(tokens))
        hidden_all = spread_hidden(hidden)
        errors_all = all_errors(raw0, error0, 1.0, 1.0)
        hidden1_all = spread_hidden(hidden1)
        errors1_all = all_errors(raw1, error1, active[0], active_row.reshape(-1, 1))
        moved_all = spread_hidden(moved)

        def home(v):
            out = jnp.zeros((fm, blk), bf16)
            for i, (d, f) in enumerate(lasts):
                own = v[:, i * blk : (i + 1) * blk]
                got = send(own, h=-d, s=f) if (d, f) != (0, 0) else own
                out = lax.dynamic_update_slice_in_dim(out, got, ((s ^ f) * nh + (h + d) % nh) * part, 0)
            return out

        sum_out = dot(hidden_all, errors_all, 1, 0) + dot(hidden1_all, errors1_all, 1, 0)
        update_out = home(sum_out.astype(bf16)).astype(f32)
        sum_in = dot(moved_all, tokens_all, 1, 0)
        update_in = home(sum_in.astype(bf16)).T.astype(f32)
        return update_in, update_out

    return local


def make_fast(n_clients, n_mp):
    nc = CORES
    ny = n_mp // nc
    nx = max(d for d in range(1, n_clients + 1) if n_clients % d == 0 and d * d <= n_clients)
    nz = n_clients // nx
    nh = nz // SIDES
    groups = [(d, t) for d in range(nh) for t in range(nx)]
    others = groups[1:]
    peers = [(g, r) for g in range(SIDES) for r in range(ny)]
    far_peers = peers[1:]
    order = [(g, k, r) for g in range(SIDES) for k in range(nc) for r in range(ny)]
    cols = [(d, f, t) for d in range(nh) for f in range(SIDES) for t in range(nx)]
    lasts = [(d, f) for d in range(nh) for f in range(SIDES)]

    def flat(h, s, x, y, c):
        return (((h % nh) * SIDES + s) * nx + x % nx) * n_mp + (y % ny) * nc + c

    def send(value, h=0, s=0, x=0, y=0, c=0):
        pairs = [
            (flat(a, b, d, e, k), flat(a + h, b ^ s, d + x, e + y, k ^ c))
            for a, b, d, e, k in itertools.product(range(nh), range(SIDES), range(nx), range(ny), range(nc))
        ]
        return lax.ppermute(value, ("clients", "mp"), pairs)

    vmem = pl.BlockSpec(memory_space=pltpu.VMEM)
    smem = pl.BlockSpec(memory_space=pltpu.SMEM)
    anyspace = pl.BlockSpec(memory_space=pl.ANY)

    def call(kernel, outs, *args, scalars=(), scratch=(), name=None):
        return pl.pallas_call(
            kernel,
            name=name,
            out_shape=[jax.ShapeDtypeStruct(*o) for o in outs],
            in_specs=[smem] * len(scalars) + [vmem] * len(args),
            out_specs=[vmem] * len(outs),
            scratch_shapes=list(scratch),
            compiler_params=pltpu.CompilerParams(vmem_limit_bytes=56 * 2**20),
        )(*scalars, *args)

    def assemble(shape, dtype, sources, moves, offsets):
        def kernel(offs, *refs):
            ins, out, sems = refs[: len(sources)], refs[len(sources)], refs[len(sources) + 1]

            def at(v):
                return pl.multiple_of(offs[v[1]], v[2]) if isinstance(v, tuple) else v

            copies = []
            for i, (a, r, c, hgt, wid, ro, co) in enumerate(moves):
                copies.append(
                    pltpu.make_async_copy(
                        ins[a].at[pl.ds(at(r), hgt), pl.ds(at(c), wid)],
                        out.at[pl.ds(ro, hgt), pl.ds(co, wid)],
                        sems.at[i],
                    )
                )
                copies[-1].start()
            for copy in copies:
                copy.wait()

        return pl.pallas_call(
            kernel,
            out_shape=jax.ShapeDtypeStruct(shape, dtype),
            in_specs=[smem] + [anyspace] * len(sources),
            out_specs=vmem,
            scratch_shapes=[pltpu.SemaphoreType.DMA((len(moves),))],
        )(offsets, *sources)

    def local(inputs, targets, local_steps, sample_counts, weight_in, weight_out):
        ci, mi = lax.axis_index("clients"), lax.axis_index("mp")
        z, x = ci // nx, ci % nx
        h, s = z // SIDES, z % SIDES
        y, c = mi // nc, mi % nc
        rows, width = inputs.shape[1:]
        rb = rows // n_mp
        half = ny * rb
        blk, fm = weight_in.shape
        ff = fm // SIDES
        part = ff // nh
        wide = len(lasts) * blk
        start = [((((h - d) % nh) * SIDES + (s ^ f)) * nx + (x - t) % nx) * blk for d, f, t in cols]
        at = {j: n * blk for n, j in enumerate(cols)}
        row_at = {o: n * rb for n, o in enumerate(order)}
        tok = inputs[0]

        def gather(own, other):
            slots = {(0, 0, 0): own}
            for d in list(range(1, nh)) + [0]:
                for f in range(SIDES):
                    if (d, f) != (0, 0):
                        slots[d, f, 0] = send((own, other)[f], h=d, s=f)
            for d in range(nh):
                for f in range(SIDES):
                    for t in range(1, nx):
                        slots[d, f, t] = send(slots[d, f, 0], x=t)
            return [slots[j] for j in cols]

        w_in = gather(
            lax.dynamic_slice_in_dim(weight_in, s * ff, ff, 1),
            lax.dynamic_slice_in_dim(weight_in, (1 - s) * ff, ff, 1),
        )
        w_out = gather(
            lax.dynamic_slice_in_dim(weight_out, s * ff, ff, 0),
            lax.dynamic_slice_in_dim(weight_out, (1 - s) * ff, ff, 0),
        )

        def row_of(r, k):
            return (((y - r) % ny) * nc + (c ^ k)) * rb

        mine = cat([lax.dynamic_slice_in_dim(tok, row_of(r, 0), rb, 0) for r in range(ny)])
        theirs = send(mine, s=1)
        theirs_far = send(theirs, c=1)
        own_rows = [(k, r) for k in range(nc) for r in range(ny)]
        offsets = jnp.stack([jnp.asarray(v, jnp.int32) for v in start + [row_of(r, k) for k, r in own_rows]])
        col = {j: ("o", n, blk) for n, j in enumerate(cols)}
        row = {kr: ("o", len(cols) + n, rb) for n, kr in enumerate(own_rows)}
        moves = []
        for j in cols:
            for k, r in own_rows:
                moves.append((0, row[k, r], col[j], rb, blk, row_at[0, k, r], at[j]))
            for k in range(nc):
                moves.append((1 + k, 0, col[j], half, blk, row_at[1, k, 0], at[j]))
        tokens = assemble((2 * rows, width), bf16, [tok, theirs, theirs_far], moves, offsets)
        wanted = assemble(
            (rb, width), bf16, [targets[0]], [(0, row[0, 0], col[j], rb, blk, 0, at[j]) for j in cols], offsets
        )
        gram = [dot(tokens[g * rows : (g + 1) * rows], tokens[g * rows : (g + 1) * rows], 1, 1).astype(bf16) for g in range(SIDES)]

        def pre_kernel(*refs):
            w, (u, pre, hid) = refs[: len(cols)], refs[len(cols) :]
            for g in range(SIDES):
                rs = pl.ds(g * rows, rows)
                acc = None
                for j, wj in zip(cols, w):
                    one = dot(u[rs, at[j] : at[j] + blk], wj[...], 1, 0)
                    acc = one if acc is None else acc + one
                pre[rs, :] = acc
                hid[rs, :] = (acc * jax.nn.sigmoid(acc)).astype(bf16)

        pre, hidden = call(
            pre_kernel, [((2 * rows, ff), f32), ((2 * rows, ff), bf16)], *w_in, tokens, name="forward"
        )

        def out_kernel(*refs):
            w, (hid, near, far) = refs[: len(cols)], refs[len(cols) :]
            for j, wj in zip(cols, w):
                for g in range(SIDES):
                    acc = dot(hid[g * rows : (g + 1) * rows, :], wj[...], 1, 0)
                    near[g * half : (g + 1) * half, at[j] : at[j] + blk] = acc[:half]
                    far[g * half : (g + 1) * half, at[j] : at[j] + blk] = acc[half:].astype(bf16)

        split = [((2 * half, width), f32), ((2 * half, width), bf16)]
        near0, far0 = call(out_kernel, split, *w_out, hidden, name="output")

        count, samples = local_steps[0], sample_counts[0]
        pair = jnp.broadcast_to(jnp.stack([samples, samples * count, count])[:, None], (3, 128))
        pair, hidden_t = lax.optimization_barrier((pair, hidden))
        pair_far = send(pair, s=1)
        total = pair + pair_far
        total = sum([send(total, x=t) for t in range(1, nx)], total)
        total = sum([send(total, h=d) for d in range(1, nh)], total)
        ntot = total[0, 0].astype(f32)
        ntau = total[1, 0].astype(f32)
        scale = ntau / (ntot * ntot)
        counts = (count, pair_far[2, 0])
        factor = [n.astype(f32) / k.astype(f32) * scale for n, k in zip((samples, pair_far[0, 0]), counts)]
        active = [(k > 1).astype(f32) for k in counts]
        weights = jnp.stack(factor + active)

        def sum_kernel(near, got, own, *pieces):
            for i, out in enumerate((own,) + pieces):
                v = near[i * rb : (i + 1) * rb, :] + got[i * rb : (i + 1) * rb, :].astype(f32)
                out[...] = v if i == 0 else v.astype(bf16)

        def swapped(j):
            return at[j[0], j[1] ^ 1, j[2]]

        def error_kernel(step):
            def kernel(wt, own, want, *refs):
                got, (e, ew) = refs[: len(far_peers)], refs[len(far_peers) :]
                by = wt[0] if step == 0 else wt[0] * wt[SIDES]
                for j in cols:
                    here = slice(at[j], at[j] + blk)
                    v = own[:, here]
                    for (g, r), piece in zip(far_peers, got):
                        a = swapped(j) if g else at[j]
                        v = v + piece[:, a : a + blk].astype(f32)
                    v = (v - want[:, here].astype(f32)) * loss_scale
                    e[:, here] = v.astype(bf16)
                    ew[:, here] = (v * by).astype(bf16)

            return kernel

        def errors(near, far, step):
            got = send(far, c=1)
            own, *pieces = call(
                sum_kernel, [((rb, width), f32)] + [((rb, width), bf16)] * len(far_peers), near, got, name="pair_sum"
            )
            got = [send(v, s=g, y=-r) for (g, r), v in zip(far_peers, pieces)]
            return call(
                error_kernel(step), [((rb, width), bf16)] * 2, own, wanted, *got, scalars=(weights,), name="error"
            )

        def spread(piece):
            out = {(0, 0, 0): piece}
            for g, r in far_peers:
                out[g, 0, (-r) % ny] = send(piece, s=g, y=-r)
            for g, r in peers:
                out[g, 1, r] = send(out[g, 0, r], c=1)
            return [out[o] for o in order]

        def place(e, pieces):
            for (g, k, r), piece in zip(order, pieces):
                rs = pl.ds(row_at[g, k, r], rb)
                if g == 0:
                    e[rs, :] = piece[...]
                else:
                    for j in cols:
                        e[rs, at[j] : at[j] + blk] = piece[:, swapped(j) : swapped(j) + blk]

        n_o, n_c = len(order), len(cols)

        def back_of(e, w, g):
            acc = None
            for j, wj in zip(cols, w):
                one = dot(e[g * rows : (g + 1) * rows, at[j] : at[j] + blk], wj[...], 1, 1)
                acc = one if acc is None else acc + one
            return acc

        def slope(back, v):
            sigma = jax.nn.sigmoid(v)
            return (back * sigma * (1.0 + v * (1.0 - sigma))).astype(bf16)

        def middle_kernel(*refs):
            pieces, w = refs[:n_o], refs[n_o : n_o + n_c]
            pre_, g0, g1, e, dpre, pre1_, hid1 = refs[n_o + n_c :]
            place(e, pieces)
            for g, gg in enumerate((g0, g1)):
                rs = pl.ds(g * rows, rows)
                d = slope(back_of(e, w, g), pre_[rs, :])
                dpre[rs, :] = d
                v = pre_[rs, :] - learn_rate * dot(gg[...], d, 1, 0)
                pre1_[rs, :] = v
                hid1[rs, :] = (v * jax.nn.sigmoid(v)).astype(bf16)

        error0, scaled0 = errors(near0, far0, 0)
        error0, dpre0, pre1, hidden1 = call(
            middle_kernel,
            [((2 * rows, width), bf16), ((2 * rows, ff), bf16), ((2 * rows, ff), f32), ((2 * rows, ff), bf16)],
            *spread(error0),
            *w_out,
            pre,
            *gram,
            name="middle",
        )

        def out1_kernel(*refs):
            w, (hid1, hid0, e, near, far) = refs[:n_c], refs[n_c:]
            for g in range(SIDES):
                rs = pl.ds(g * rows, rows)
                cross = dot(hid1[rs, :], hid0[rs, :], 1, 1).astype(bf16)
                for j, wj in zip(cols, w):
                    here = slice(at[j], at[j] + blk)
                    acc = dot(hid1[rs, :], wj[...], 1, 0) - learn_rate * dot(cross, e[rs, here], 1, 0)
                    near[g * half : (g + 1) * half, here] = acc[:half]
                    far[g * half : (g + 1) * half, here] = acc[half:].astype(bf16)

        near1, far1 = call(out1_kernel, split, *w_out, hidden1, hidden, error0, name="output1")
        error1, scaled1 = errors(near1, far1, 1)

        def end_kernel(wt, *refs):
            pieces, w = refs[:n_o], refs[n_o : n_o + n_c]
            e0, hid0, pre1_, dpre, e1, moved = refs[n_o + n_c :]
            place(e1, pieces)
            for g in range(SIDES):
                rs = pl.ds(g * rows, rows)
                both = dot(e1[rs, :], e0[rs, :], 1, 1).astype(bf16)
                back = back_of(e1, w, g) - learn_rate * dot(both, hid0[rs, :], 1, 0)
                d = slope(back, pre1_[rs, :]).astype(f32)
                v = (dpre[rs, :].astype(f32) + wt[SIDES + g] * d) * wt[g]
                moved[:, g * rows : (g + 1) * rows] = v.T.astype(bf16)

        error1, moved = call(
            end_kernel,
            [((2 * rows, width), bf16), ((ff, 2 * rows), bf16)],
            *spread(error1),
            *w_out,
            error0,
            hidden,
            pre1,
            dpre0,
            scalars=(weights,),
            name="end",
        )

        def across(piece):
            return [
                send(cat([piece[:, at[e, f, (-t) % nx] : at[e, f, (-t) % nx] + blk] for e, f in lasts], 1), h=d, x=t)
                for d, t in others
            ]

        def spread_hidden(v):
            near = {}
            for d in range(nh):
                own = lax.dynamic_slice_in_dim(v, ((h + d) % nh) * part, part, 0)
                near[d, 0] = send(own, h=d) if d else own
            for d in range(nh):
                for t in range(1, nx):
                    near[d, t] = send(near[d, 0], x=t)
            return [near[b] for b in groups]

        def final_kernel(steps, weighted):
            n_g = len(groups)

            def kernel(*refs):
                if weighted:
                    wt, refs = refs[0], refs[1:]
                left, refs = refs[: steps * n_g], refs[steps * n_g :]
                near, refs = refs[:steps], refs[steps:]
                got, refs = refs[:n_o], refs[n_o:]
                outs, (r, acc) = refs[: len(lasts)], refs[len(lasts) :]
                for st in range(steps):
                    for b, (d, t) in enumerate(groups):
                        if b == 0:
                            for g in range(SIDES):
                                rs = pl.ds(g * rows, rows)
                                for i, (e, f) in enumerate(lasts):
                                    v = near[st][rs, at[e, f, 0] : at[e, f, 0] + blk]
                                    if weighted:
                                        by = wt[g] * wt[SIDES + g] if st else wt[g]
                                        v = (v.astype(f32) * by).astype(bf16)
                                    r[rs, i * blk : (i + 1) * blk] = v
                        else:
                            first = (st * (n_g - 1) + b - 1) * rb
                            for (g, k, q), piece in zip(order, got):
                                for i, (e, f) in enumerate(lasts):
                                    n = lasts.index(((e - d) % nh, f ^ g))
                                    r[pl.ds(row_at[g, k, q], rb), i * blk : (i + 1) * blk] = piece[
                                        first : first + rb, n * blk : (n + 1) * blk
                                    ]
                        one = dot(left[st * n_g + b][...], r[...], 1, 0)
                        if st == 0 and b == 0:
                            acc[...] = one
                        else:
                            acc[...] += one
                for i, out in enumerate(outs):
                    out[...] = acc[:, i * blk : (i + 1) * blk].astype(bf16)

            return kernel

        def final(left, near, got, scalars, name):
            return call(
                final_kernel(len(near), bool(scalars)),
                [((part, blk), bf16)] * len(lasts),
                *left,
                *near,
                *got,
                scalars=scalars,
                scratch=[pltpu.VMEM((2 * rows, wide), bf16), pltpu.VMEM((part, wide), f32)],
                name=name,
            )

        def home(pieces, turned, name):
            got = [send(v, h=-d, s=f) if (d, f) != (0, 0) else v for (d, f), v in zip(lasts, pieces)]
            places = jnp.stack([((s ^ f) * nh + (h + d) % nh) * part for d, f in lasts]).astype(jnp.int32)

            def kernel(offs, *refs):
                ins, out = refs[: len(lasts)], refs[len(lasts)]
                into = refs[-1] if turned else out
                for i, v in enumerate(ins):
                    into[pl.ds(pl.multiple_of(offs[i], 16), part), :] = v[...].astype(f32)
                if turned:
                    out[...] = into[...].T

            shape = (blk, fm) if turned else (fm, blk)
            scratch = [pltpu.VMEM((fm, blk), f32)] if turned else []
            return call(kernel, [(shape, f32)], *got, scalars=(places,), scratch=scratch, name=name)[0]

        piece_u, _ = lax.optimization_barrier((tokens[:rb], near0))
        hidden_all = spread_hidden(lax.optimization_barrier((hidden, near0))[0].T)
        across_u = cat(across(piece_u))
        tokens_all = spread(lax.optimization_barrier((across_u, error0))[0])
        hidden1_all = spread_hidden(hidden1.T)
        across_e = across(scaled0) + across(scaled1)
        errors_all = spread(lax.optimization_barrier((cat(across_e), error1))[0])
        moved_all = spread_hidden(moved)

        out_pieces = final(hidden_all + hidden1_all, [error0, error1], errors_all, (weights,), "sum_out")
        in_pieces = final(moved_all, [tokens], tokens_all, (), "sum_in")
        update_out = home(out_pieces, False, "home_out")
        update_in = home(in_pieces, True, "home_in")
        return update_in, update_out

    return local


def solution(mesh):
    in_specs = (
        P("clients", None, None),
        P("clients", None, None),
        P("clients"),
        P("clients"),
        P("clients", "mp"),
        P("mp", "clients"),
    )
    out_specs = (P("clients", "mp"), P("mp", "clients"))
    sizes = mesh.shape["clients"], mesh.shape["mp"]
    plain, fast = make_plain(*sizes), make_fast(*sizes)

    def body(*args):
        tiled = args[4].shape[0] % 128 == 0 and args[4].shape[1] % 256 == 0
        return (fast if tiled else plain)(*args)

    return jax.shard_map(body, mesh=mesh, in_specs=in_specs, out_specs=out_specs, check_vma=False)
```
